32 devices in a mesh: ep: 8 (over z, x), dp: 4 (over y, core).
Axes of the slice: x: 2, y: 2, z: 4, core: 2. Of those that a mesh axis runs over, the one named last changes fastest.
Arguments:
- residual: bfloat16 [4096, 2880], P(('ep', 'dp')), may hold values from -400 to 400, as said below
- norm_gain: float32 [2880], replicated, may hold values from 0.25 to 1.75
- router_weight: bfloat16 [2880, 32], replicated, may hold values from -0.109375 to 0.109375
- out_grad: bfloat16 [4096, 2880], P(('ep', 'dp')), may hold values from -6 to 6
- expert_ids: int32 [4096, 4], P(('ep', 'dp')), may hold values from 0 to 31, all different within a row; in each aligned block of 128 rows (0 to 127, 128 to 255, ...) at most 24 rows name the same one
- hidden: bfloat16 [32, 768, 1440], P(('ep', 'dp')), may hold values from -0.3125 to 0.3125
- down_weight: bfloat16 [32, 1440, 2880], P(('ep', 'dp')), may hold values from -0.15625 to 0.15625
Outputs:
- hidden_grad: bfloat16 [32, 768, 1440], P(('ep', 'dp'))
- down_weight_grad: bfloat16 [32, 1440, 2880], P(('ep', 'dp'))
- residual_grad: bfloat16 [4096, 2880], P(('ep', 'dp'))
- router_grad: float32 [2880, 32], replicated
- gain_grad: float32 [2880], replicated
The draws below stay inside these ranges and needn't reach their ends.
Inputs may be any that keep to these rules, and one draw needn't show every extreme that they name: `expert_ids`: in the tokens of one device no expert is named more than 24 times, a bound that some block reaches. `residual`: Real-valued entries.
All inputs are finite; a program needn't handle non-finite values.
Results may differ from the reference program's by a relative error of at most 0.0085.
Values may be sent and summed in bfloat16 or wider, within the bound.
No kernel may reach another device: no remote copies, remote signals or barrier semaphores. Data moves between devices by JAX's collectives and lax.ppermute only.
A program may use at most 128 MiB of HBM per device.

```python
import math
import jax
import jax.numpy as jnp
import numpy as np
from jax import lax

D = 2880
TOPK = 4
FF = 1440
TOK_DEV = 128
EXPERTS = 32
TOKENS = 4096
CAP = 24
SLOTS = 768
N_EP = 8
N_DP = 4


def draw_residual(key, part):
    key_rows, key_cols, key_base = jax.random.split(key, 3)
    row_scale = jnp.exp(jax.random.uniform(key_rows, (TOKENS, 1), jnp.float32, 0.0, math.log(10.0)))
    column_scale = jnp.exp(jax.random.uniform(key_cols, (1, D), jnp.float32, 0.0, math.log(10.0)))
    base = jax.random.truncated_normal(key_base, -3.5, 3.5, (TOKENS, D), jnp.float32)
    return (base * row_scale * column_scale).astype(jnp.bfloat16)


def shard_levels(own_key, dims, pieces, least, high):
    loudness = 1.0
    for dim, shards_of in pieces:
        draws = jax.random.uniform(jax.random.fold_in(jax.random.fold_in(own_key, 6), dim), (shards_of,), jnp.float32, least / len(pieces), high / len(pieces))
        loudness = loudness * jnp.repeat(jnp.exp(draws), dims[dim] // shards_of).reshape((-1,) + (1,) * (len(dims) - 1 - dim))
    return loudness


def deal_out(key, own, number, rows, number_of, top, reach, skew):
    sequence = jax.random.permutation(key, number_of)
    crowded, ordinary = load_shares(number_of, rows * top, reach, skew, True), load_shares(number_of, rows * top, reach, skew, False)
    places = jnp.arange(number_of)

    def named(tallies, turn):
        used = int((tallies > 0).sum())
        fixed = max(1, used // 4)
        passed = fixed + (places - fixed + turn * (used - fixed)) % max(1, number_of - fixed)
        return jnp.zeros((number_of,), jnp.int32).at[sequence[jnp.where(places < fixed, places, passed)]].set(jnp.asarray(tallies, jnp.int32))

    tallies = jnp.where(number % 4 == 0, named(crowded, number // 4), named(ordinary, number - number // 4 - 1))
    mixed = jax.random.permutation(jax.random.fold_in(own, 3), number_of)
    source_of, sink = mixed[0:number_of // 2 * 2:2], mixed[1:number_of // 2 * 2:2]
    slack = jnp.minimum(tallies[source_of] - 1, reach - tallies[sink]) // 2
    slack = jnp.where((source_of == sequence[0]) | (sink == sequence[0]) | (tallies[sink] == 0), 0, jnp.maximum(slack, 0))
    passed = jax.random.randint(jax.random.fold_in(own, 4), (number_of // 2,), 0, 1 << 20) % (slack + 1)
    tallies = tallies.at[source_of].add(-passed).at[sink].add(passed)
    items = jnp.searchsorted(jnp.cumsum(tallies), jnp.arange(rows * top), side="right").astype(jnp.int32)
    grid = items.reshape(top, rows).T
    grid = grid[jax.random.permutation(jax.random.fold_in(own, 1), rows)]
    turn = jax.random.randint(jax.random.fold_in(own, 2), (rows, 1), 0, top)
    return jnp.take_along_axis(grid, (jnp.arange(top)[None, :] + turn) % top, axis=1)


def load_shares(count, total, reach, slope, full):
    weights = [(1 << 20) // math.isqrt(standing ** slope) + 1 for standing in range(1, count + 1)]
    largest = reach if full else min(reach, max(-(-total // count), total * weights[0] // sum(weights)))
    least = 1 if total - largest >= count - 1 else 0
    given, rest = [largest] + [least] * (count - 1), total - largest - least * (count - 1)
    while rest > 0:
        free = [i for i in range(1, count) if given[i] < largest] or [i for i in range(1, count) if given[i] < reach]
        mass, remaining = sum([weights[i] for i in free]), rest
        for i in free:
            addition = min(reach - given[i], max(1, remaining * weights[i] // mass), rest)
            given[i] = given[i] + addition
            rest = rest - addition
    return np.array(given)


def scatter_about(rng, shape, scale, limit, shards=(), held_as=jnp.bfloat16):
    level = shard_levels(rng, shape, shards, -0.22, 0.18) if shards else 1.0
    values = jax.random.normal(rng, shape, jnp.float32) * scale * level
    return jnp.minimum(jnp.maximum(values, -limit), limit).astype(held_as)


def setup_inputs(seed: int = 0) -> dict:
    streams_of = jax.random.split(jax.random.key(seed), 8)
    residual = draw_residual(jax.random.fold_in(streams_of[7], 71), 0)
    norm_gain = jnp.clip(1.0 + 0.15 * jax.random.normal(streams_of[1], (D,), jnp.float32), 0.25, 1.75)
    router_weight = scatter_about(streams_of[2], (D, EXPERTS), D ** -0.5, 0.109375)
    out_grad = scatter_about(streams_of[3], (TOKENS, D), 1.0, 6.0, ((0, 32),))
    expert_ids_keys = jax.random.split(jax.random.fold_in(streams_of[4], 1), TOKENS // TOK_DEV)
    expert_ids_turns = jax.random.permutation(jax.random.fold_in(streams_of[4], 3), TOKENS // TOK_DEV)
    expert_ids = jax.vmap(lambda own, number: deal_out(jax.random.fold_in(streams_of[4], 2), own, number, TOK_DEV, EXPERTS, TOPK, CAP, 2))(expert_ids_keys, expert_ids_turns).reshape((TOKENS, TOPK))
    hidden = scatter_about(streams_of[5], (EXPERTS, SLOTS, FF), 0.05, 0.3125, ((0, 32),))
    down_weight = scatter_about(streams_of[6], (EXPERTS, FF, D), FF ** -0.5, 0.15625, ((0, 32),))
    return {"residual": residual, "norm_gain": norm_gain, "router_weight": router_weight, "out_grad": out_grad, "expert_ids": expert_ids, "hidden": hidden, "down_weight": down_weight}


def expert_step(packed):
    sent_grad, sent_prob, hidden_rows, weight = packed
    inner = lax.dot_general(sent_grad, weight, (((1,), (1,)), ((), ())), preferred_element_type=jnp.float32)
    slot_score = lax.optimization_barrier(jnp.sum(inner * hidden_rows.astype(jnp.float32), -1))
    weight_col = sent_prob.astype(jnp.float32)[:, None]
    hidden_grad = (weight_col * inner).astype(jnp.bfloat16)
    scaled = (weight_col * sent_grad.astype(jnp.float32)).astype(jnp.bfloat16)
    weight_grad = lax.dot_general(hidden_rows, scaled, (((0,), (0,)), ((), ())), preferred_element_type=jnp.float32)
    return (slot_score, hidden_grad, weight_grad.astype(jnp.bfloat16))

def reference(residual, norm_gain, router_weight, out_grad, expert_ids, hidden, down_weight):
    sources = N_EP * N_DP
    floated = residual.astype(jnp.float32)
    inverse = lax.rsqrt(lax.optimization_barrier(jnp.mean(floated * floated, -1, keepdims=True)) + 1e-05)
    unit = floated * inverse
    normed = (unit * norm_gain).astype(jnp.bfloat16)
    logits = jnp.dot(normed, router_weight, preferred_element_type=jnp.float32)
    picked = jnp.take_along_axis(logits, expert_ids, 1)
    expo = jnp.exp(picked)
    prob = expo / lax.optimization_barrier(jnp.sum(expo, -1, keepdims=True))
    flat_ids = expert_ids.reshape(sources, TOK_DEV * TOPK)
    onehot = (flat_ids[:, :, None] == jnp.arange(EXPERTS, dtype=jnp.int32)[None, None, :]).astype(jnp.int32)
    before = jnp.cumsum(onehot, 1) - onehot
    slot_rank = lax.optimization_barrier(jnp.sum(before * onehot, -1))
    source_idx = jnp.arange(sources, dtype=jnp.int32)[:, None]
    place = (flat_ids * SLOTS + source_idx * CAP + slot_rank).reshape(-1).astype(jnp.int32)
    repeated = jnp.repeat(out_grad, TOPK, axis=0)
    sent_grad = jnp.zeros((EXPERTS * SLOTS, D), jnp.bfloat16).at[place].set(repeated).reshape(EXPERTS, SLOTS, D)
    sent_prob = jnp.zeros((EXPERTS * SLOTS,), jnp.bfloat16).at[place].set(prob.astype(jnp.bfloat16).reshape(-1)).reshape(EXPERTS, SLOTS)
    slot_score, hidden_grad, down_weight_grad = lax.map(expert_step, (sent_grad, sent_prob, hidden, down_weight))
    score = slot_score.reshape(-1)[place].reshape(TOKENS, TOPK)
    pick_grad = prob * (score - lax.optimization_barrier(jnp.sum(prob * score, -1, keepdims=True)))
    match = expert_ids[:, :, None] == jnp.arange(EXPERTS, dtype=jnp.int32)[None, None, :]
    logit_grad = lax.optimization_barrier(jnp.sum(jnp.where(match, pick_grad[:, :, None], jnp.float32(0.0)), 1))
    router_grad = jnp.dot(normed.astype(jnp.float32).T, logit_grad, precision=lax.Precision.HIGHEST)
    normed_grad = jnp.dot(logit_grad, router_weight.astype(jnp.float32).T, precision=lax.Precision.HIGHEST)
    gain_grad = lax.optimization_barrier(jnp.sum(normed_grad * unit, 0))
    upper = normed_grad * norm_gain
    residual_grad = (inverse * (upper - unit * lax.optimization_barrier(jnp.mean(upper * unit, -1, keepdims=True)))).astype(jnp.bfloat16)
    return (hidden_grad, down_weight_grad, residual_grad, router_grad, gain_grad)
```

```python
import jax
import jax.numpy as jnp
from jax import lax
from jax.sharding import PartitionSpec as P

AXES = ("ep", "dp")


def on_device(residual, norm_gain, router_weight, out_grad, expert_ids, hidden, down_weight):
    tokens_here, width = residual.shape
    experts = router_weight.shape[1]
    slots = hidden.shape[1]
    capacity = slots // experts
    me = lax.axis_index(AXES)

    floated = residual.astype(jnp.float32)
    inverse = lax.rsqrt(jnp.mean(floated * floated, -1, keepdims=True) + 1e-05)
    unit = floated * inverse
    normed = (unit * norm_gain).astype(jnp.bfloat16)
    logits = jnp.dot(normed, router_weight, preferred_element_type=jnp.float32)
    names = jnp.arange(experts, dtype=jnp.int32)
    chosen = jnp.any(expert_ids[:, :, None] == names[None, None, :], 1)
    expo = jnp.where(chosen, jnp.exp(jnp.where(chosen, logits, 0.0)), 0.0)
    prob = expo / jnp.sum(expo, -1, keepdims=True)

    steps = jnp.arange(tokens_here, dtype=jnp.int32)
    earlier = (steps[:, None] > steps[None, :]).astype(jnp.bfloat16)
    rank = jnp.dot(earlier, chosen.astype(jnp.bfloat16), preferred_element_type=jnp.float32)
    owned = jnp.where(chosen, rank.astype(jnp.int32), -1).T
    select = owned[:, None, :] == jnp.arange(capacity, dtype=jnp.int32)[None, :, None]

    spare = -(width + experts) % 128
    packed = jnp.concatenate(
        [
            out_grad,
            prob.astype(jnp.bfloat16),
            jnp.zeros((tokens_here, spare), jnp.bfloat16),
        ],
        1,
    )
    onehot = select.astype(jnp.bfloat16).reshape(experts * capacity, tokens_here)
    send = jnp.dot(onehot, packed, preferred_element_type=jnp.float32).astype(jnp.bfloat16)
    got = lax.all_to_all(
        send.reshape(experts, capacity, -1), AXES, split_axis=0, concat_axis=0, tiled=True
    ).reshape(slots, -1)

    got_rows = got[:, :width]
    mine = jnp.arange(experts, dtype=jnp.int32)[None, :] == me
    tail = got[:, width : width + experts].astype(jnp.float32)
    weight_col = jnp.sum(jnp.where(mine, tail, 0.0), 1, keepdims=True)
    hidden_rows = hidden[0]
    weight = down_weight[0]
    inner = lax.dot_general(
        got_rows, weight, (((1,), (1,)), ((), ())), preferred_element_type=jnp.float32
    )
    slot_score = jnp.sum(inner * hidden_rows.astype(jnp.float32), -1)
    hidden_grad = (weight_col * inner).astype(jnp.bfloat16)
    scaled = (weight_col * got_rows.astype(jnp.float32)).astype(jnp.bfloat16)
    weight_grad = lax.dot_general(
        hidden_rows, scaled, (((0,), (0,)), ((), ())), preferred_element_type=jnp.float32
    )

    came_back = lax.all_to_all(
        slot_score.reshape(experts, capacity), AXES, split_axis=0, concat_axis=0, tiled=True
    )
    score = jnp.sum(jnp.where(select, came_back[:, :, None], 0.0), 1).T
    logit_grad = prob * (score - jnp.sum(prob * score, -1, keepdims=True))

    local_router = lax.dot_general(
        logit_grad,
        normed.astype(jnp.float32),
        (((0,), (0,)), ((), ())),
        precision=lax.Precision.HIGHEST,
    )
    pieces = lax.all_to_all(local_router, AXES, split_axis=0, concat_axis=0, tiled=True)
    total = jnp.sum(pieces, 0, keepdims=True)
    router_rows = lax.all_to_all(
        jnp.broadcast_to(total, (experts, width)), AXES, split_axis=0, concat_axis=0, tiled=True
    )
    gain_grad = jnp.sum(router_rows * router_weight.T.astype(jnp.float32), 0) / norm_gain

    normed_grad = jnp.dot(
        logit_grad, router_weight.astype(jnp.float32).T, precision=lax.Precision.HIGHEST
    )
    upper = normed_grad * norm_gain
    residual_grad = (inverse * (upper - unit * jnp.mean(upper * unit, -1, keepdims=True))).astype(
        jnp.bfloat16
    )
    return (
        hidden_grad[None],
        weight_grad.astype(jnp.bfloat16)[None],
        residual_grad,
        router_rows.T,
        gain_grad,
    )


def solution(mesh):
    return jax.shard_map(
        on_device,
        mesh=mesh,
        in_specs=(
            P(AXES, None),
            P(),
            P(),
            P(AXES, None),
            P(AXES, None),
            P(AXES, None, None),
            P(AXES, None, None),
        ),
        out_specs=(
            P(AXES, None, None),
            P(AXES, None, None),
            P(AXES, None),
            P(),
            P(),
        ),
        check_vma=False,
    )
```

```python
import math

import jax
import jax.numpy as jnp
from jax import lax
from jax.sharding import Mesh
from jax.sharding import PartitionSpec as P

AXES = ("plane", "row", "dp")
IN_PLANE = ("row", "dp")


def on_device(residual, norm_gain, router_weight, out_grad, expert_ids, hidden, down_weight):
    tokens_here, width = residual.shape
    experts = router_weight.shape[1]
    slots = hidden.shape[1]
    capacity = slots // experts
    me = lax.axis_index(AXES)

    floated = residual.astype(jnp.float32)
    inverse = lax.rsqrt(jnp.mean(floated * floated, -1, keepdims=True) + 1e-05)
    unit = floated * inverse
    normed = (unit * norm_gain).astype(jnp.bfloat16)
    logits = jnp.dot(normed, router_weight, preferred_element_type=jnp.float32)
    names = jnp.arange(experts, dtype=jnp.int32)
    chosen = jnp.any(expert_ids[:, :, None] == names[None, None, :], 1)
    expo = jnp.where(chosen, jnp.exp(jnp.where(chosen, logits, 0.0)), 0.0)
    prob = expo / jnp.sum(expo, -1, keepdims=True)

    steps = jnp.arange(tokens_here, dtype=jnp.int32)
    earlier = (steps[:, None] > steps[None, :]).astype(jnp.bfloat16)
    rank = jnp.dot(earlier, chosen.astype(jnp.bfloat16), preferred_element_type=jnp.float32)
    owned = jnp.where(chosen, rank.astype(jnp.int32), -1).T
    select = owned[:, None, :] == jnp.arange(capacity, dtype=jnp.int32)[None, :, None]

    planes = lax.axis_size("plane")
    here = lax.axis_index("plane")
    near = experts // planes
    spare = -(width + 2 * experts) % 128
    packed = jnp.concatenate(
        [
            out_grad,
            prob.astype(jnp.bfloat16),
            owned.T.astype(jnp.bfloat16),
            jnp.zeros((tokens_here, spare), jnp.bfloat16),
        ],
        1,
    )
    onward = [((i + 1) % planes, i) for i in range(planes)]
    blocks = [packed]
    for _ in range(planes - 1):
        blocks.append(lax.ppermute(blocks[-1], "plane", onward))
    got = jnp.zeros((slots, packed.shape[1]), jnp.bfloat16)
    made = None
    for j, block in enumerate(blocks):
        if made is not None:
            block, _ = lax.optimization_barrier((block, made))
        ids = block[:, width + experts : width + 2 * experts].T
        ids = lax.dynamic_slice_in_dim(ids, here * near, near, 0).astype(jnp.int32)
        picks = ids[:, None, :] == jnp.arange(capacity, dtype=jnp.int32)[None, :, None]
        onehot = picks.astype(jnp.bfloat16).reshape(near * capacity, tokens_here)
        send = jnp.dot(onehot, block, preferred_element_type=jnp.float32).astype(jnp.bfloat16)
        made = send
        rows = lax.all_to_all(
            send.reshape(near, capacity, -1), IN_PLANE, split_axis=0, concat_axis=0, tiled=True
        ).reshape(near * capacity, -1)
        source = (here + j) % planes
        got = lax.dynamic_update_slice(got, rows, (source * near * capacity, 0))

    got_rows = got[:, :width]
    mine = jnp.arange(experts, dtype=jnp.int32)[None, :] == me
    tail = got[:, width : width + experts].astype(jnp.float32)
    weight_col = jnp.sum(jnp.where(mine, tail, 0.0), 1, keepdims=True)
    hidden_rows = hidden[0]
    weight = down_weight[0]
    inner = lax.dot_general(
        got_rows, weight, (((1,), (1,)), ((), ())), preferred_element_type=jnp.float32
    )
    slot_score = jnp.sum(inner * hidden_rows.astype(jnp.float32), -1)
    hidden_grad = (weight_col * inner).astype(jnp.bfloat16)
    scaled = (weight_col * got_rows.astype(jnp.float32)).astype(jnp.bfloat16)
    weight_grad = lax.dot_general(
        hidden_rows, scaled, (((0,), (0,)), ((), ())), preferred_element_type=jnp.float32
    )

    came_back = lax.all_to_all(
        slot_score, AXES, split_axis=0, concat_axis=0, tiled=True
    ).reshape(experts, capacity)
    score = jnp.sum(jnp.where(select, came_back[:, :, None], 0.0), 1).T
    logit_grad = prob * (score - jnp.sum(prob * score, -1, keepdims=True))

    local_router = lax.dot_general(
        logit_grad,
        normed.astype(jnp.float32),
        (((0,), (0,)), ((), ())),
        precision=lax.Precision.HIGHEST,
    )
    pieces = lax.all_to_all(local_router, AXES, split_axis=0, concat_axis=0, tiled=True)
    total = jnp.sum(pieces, 0).astype(jnp.bfloat16)
    fold = math.gcd(width, 2)
    router_rows = lax.all_to_all(
        jnp.broadcast_to(total.reshape(1, fold, -1), (experts, fold, width // fold)),
        AXES,
        split_axis=0,
        concat_axis=0,
        tiled=True,
    )
    router_rows = router_rows.reshape(experts, width).astype(jnp.float32)
    gain_grad = jnp.sum(router_rows * router_weight.T.astype(jnp.float32), 0) / norm_gain

    normed_grad = jnp.dot(
        logit_grad, router_weight.astype(jnp.float32).T, precision=lax.Precision.HIGHEST
    )
    upper = normed_grad * norm_gain
    residual_grad = (inverse * (upper - unit * jnp.mean(upper * unit, -1, keepdims=True))).astype(
        jnp.bfloat16
    )
    return (
        hidden_grad[None],
        weight_grad.astype(jnp.bfloat16)[None],
        residual_grad,
        router_rows.T,
        gain_grad,
    )


def solution(mesh):
    parts = math.gcd(mesh.shape["ep"], mesh.shape["dp"])
    mesh = Mesh(mesh.devices.reshape(parts, -1, mesh.shape["dp"]), AXES)
    return jax.shard_map(
        on_device,
        mesh=mesh,
        in_specs=(
            P(AXES, None),
            P(),
            P(),
            P(AXES, None),
            P(AXES, None),
            P(AXES, None, None),
            P(AXES, None, None),
        ),
        out_specs=(
            P(AXES, None, None),
            P(AXES, None, None),
            P(AXES, None),
            P(),
            P(),
        ),
        check_vma=False,
    )
```

```python
import math

import jax
import jax.numpy as jnp
from jax import lax
from jax.sharding import Mesh
from jax.sharding import PartitionSpec as P

AXES = ("plane", "row", "dp")
IN_PLANE = ("row", "dp")


def on_device(residual, norm_gain, router_weight, out_grad, expert_ids, hidden, down_weight):
    tokens_here, width = residual.shape
    experts = router_weight.shape[1]
    slots = hidden.shape[1]
    capacity = slots // experts
    me = lax.axis_index(AXES)

    floated = residual.astype(jnp.float32)
    inverse = lax.rsqrt(jnp.mean(floated * floated, -1, keepdims=True) + 1e-05)
    unit = floated * inverse
    normed = (unit * norm_gain).astype(jnp.bfloat16)
    logits = jnp.dot(normed, router_weight, preferred_element_type=jnp.float32)
    names = jnp.arange(experts, dtype=jnp.int32)
    chosen = jnp.any(expert_ids[:, :, None] == names[None, None, :], 1)
    expo = jnp.where(chosen, jnp.exp(jnp.where(chosen, logits, 0.0)), 0.0)
    prob = expo / jnp.sum(expo, -1, keepdims=True)

    steps = jnp.arange(tokens_here, dtype=jnp.int32)
    earlier = (steps[:, None] > steps[None, :]).astype(jnp.bfloat16)
    rank = jnp.dot(earlier, chosen.astype(jnp.bfloat16), preferred_element_type=jnp.float32)
    owned = jnp.where(chosen, rank.astype(jnp.int32), -1).T
    select = owned[:, None, :] == jnp.arange(capacity, dtype=jnp.int32)[None, :, None]

    planes = lax.axis_size("plane")
    here = lax.axis_index("plane")
    near = experts // planes
    spare = -(width + 2 * experts) % 128
    packed = jnp.concatenate(
        [
            out_grad,
            prob.astype(jnp.bfloat16),
            owned.T.astype(jnp.bfloat16),
            jnp.zeros((tokens_here, spare), jnp.bfloat16),
        ],
        1,
    )
    onward = [((i + 1) % planes, i) for i in range(planes)]
    cut = -(-packed.shape[1] // 256) * 128
    halves = [(packed[:, :cut], packed[:, cut:])]
    for _ in range(planes - 1):
        halves.append(tuple(lax.ppermute(half, "plane", onward) for half in halves[-1]))
    blocks = [packed] + [jnp.concatenate(pair, 1) for pair in halves[1:]]
    got = jnp.zeros((slots, packed.shape[1]), jnp.bfloat16)
    made = None
    for j, block in enumerate(blocks):
        if made is not None:
            block, _ = lax.optimization_barrier((block, made))
        ids = block[:, width + experts : width + 2 * experts].T
        ids = lax.dynamic_slice_in_dim(ids, here * near, near, 0).astype(jnp.int32)
        picks = ids[:, None, :] == jnp.arange(capacity, dtype=jnp.int32)[None, :, None]
        onehot = picks.astype(jnp.bfloat16).reshape(near * capacity, tokens_here)
        send = jnp.dot(onehot, block, preferred_element_type=jnp.float32).astype(jnp.bfloat16)
        made = send
        rows = lax.all_to_all(
            send.reshape(near, capacity, -1), IN_PLANE, split_axis=0, concat_axis=0, tiled=True
        ).reshape(near * capacity, -1)
        source = (here + j) % planes
        got = lax.dynamic_update_slice(got, rows, (source * near * capacity, 0))

    got_rows = got[:, :width]
    mine = jnp.arange(experts, dtype=jnp.int32)[None, :] == me
    tail = got[:, width : width + experts].astype(jnp.float32)
    weight_col = jnp.sum(jnp.where(mine, tail, 0.0), 1, keepdims=True)
    hidden_rows = hidden[0]
    weight = down_weight[0]
    inner = lax.dot_general(
        got_rows, weight, (((1,), (1,)), ((), ())), preferred_element_type=jnp.float32
    )
    slot_score = jnp.sum(inner * hidden_rows.astype(jnp.float32), -1)
    hidden_grad = (weight_col * inner).astype(jnp.bfloat16)
    scaled = (weight_col * got_rows.astype(jnp.float32)).astype(jnp.bfloat16)
    weight_grad = lax.dot_general(
        hidden_rows, scaled, (((0,), (0,)), ((), ())), preferred_element_type=jnp.float32
    )

    came_back = lax.all_to_all(
        slot_score, AXES, split_axis=0, concat_axis=0, tiled=True
    ).reshape(experts, capacity)
    score = jnp.sum(jnp.where(select, came_back[:, :, None], 0.0), 1).T
    logit_grad = prob * (score - jnp.sum(prob * score, -1, keepdims=True))

    local_router = lax.dot_general(
        logit_grad,
        normed.astype(jnp.float32),
        (((0,), (0,)), ((), ())),
        precision=lax.Precision.HIGHEST,
    )
    pieces = lax.all_to_all(local_router, AXES, split_axis=0, concat_axis=0, tiled=True)
    total = jnp.sum(pieces, 0).astype(jnp.bfloat16)
    fold = math.gcd(width, 2)
    router_rows = lax.all_to_all(
        jnp.broadcast_to(total.reshape(1, fold, -1), (experts, fold, width // fold)),
        AXES,
        split_axis=0,
        concat_axis=0,
        tiled=True,
    )
    router_rows = router_rows.reshape(experts, width).astype(jnp.float32)
    gain_grad = jnp.sum(router_rows * router_weight.T.astype(jnp.float32), 0) / norm_gain

    normed_grad = jnp.dot(
        logit_grad, router_weight.astype(jnp.float32).T, precision=lax.Precision.HIGHEST
    )
    upper = normed_grad * norm_gain
    residual_grad = (inverse * (upper - unit * jnp.mean(upper * unit, -1, keepdims=True))).astype(
        jnp.bfloat16
    )
    return (
        hidden_grad[None],
        weight_grad.astype(jnp.bfloat16)[None],
        residual_grad,
        router_rows.T,
        gain_grad,
    )


def solution(mesh):
    parts = math.gcd(mesh.shape["ep"], mesh.shape["dp"])
    mesh = Mesh(mesh.devices.reshape(parts, -1, mesh.shape["dp"]), AXES)
    return jax.shard_map(
        on_device,
        mesh=mesh,
        in_specs=(
            P(AXES, None),
            P(),
            P(),
            P(AXES, None),
            P(AXES, None),
            P(AXES, None, None),
            P(AXES, None, None),
        ),
        out_specs=(
            P(AXES, None, None),
            P(AXES, None, None),
            P(AXES, None),
            P(),
            P(),
        ),
        check_vma=False,
    )
```
